256 devices in a mesh: seq: 32 (over z, x), tp: 8 (over y, core).
Axes of the slice: x: 4, y: 4, z: 8, core: 2. Of those that a mesh axis runs over, the one named last changes fastest.
Arguments:
- hidden: bfloat16 [8192, 8192], P('seq', 'tp'), may hold values from -6 to 6
- query_base: bfloat16 [8192, 4096], P('seq', 'tp'), may hold values from -150 to 150
- rotated_key_cache: bfloat16 [8192, 1024], P('seq', 'tp'), may hold values from -7 to 7
- frozen_value_base: bfloat16 [8192, 1024], P('seq', 'tp'), may hold values from -6 to 6
- output_cotangent: bfloat16 [8192, 4096], P('seq', 'tp'), may hold values from -0.9 to 0.9
- qdown_mean: float32 [16, 8192], P(None, 'tp'), may hold values from -0.0625 to 0.0625
- qdown_sigma: float32 [16, 8192], P(None, 'tp'), may hold values from 0.004 to 0.012
- qdown_noise: float32 [16, 8192], P(None, 'tp'), may hold values from -4 to 4
- qup_mean: float32 [16, 4096], P(None, 'tp'), may hold values from -1.5 to 1.5
- qup_sigma: float32 [16, 4096], P(None, 'tp'), may hold values from 0.08 to 0.25
- qup_noise: float32 [16, 4096], P(None, 'tp'), may hold values from -4 to 4
- vdown_mean: float32 [16, 8192], P(None, 'tp'), may hold values from -0.0625 to 0.0625
- vdown_sigma: float32 [16, 8192], P(None, 'tp'), may hold values from 0.004 to 0.012
- vdown_noise: float32 [16, 8192], P(None, 'tp'), may hold values from -4 to 4
- value_up_mean: float32 [16, 1024], P(None, 'tp'), may hold values from -1.5 to 1.5
- value_up_deviation: float32 [16, 1024], P(None, 'tp'), may hold values from 0.08 to 0.25
- value_up_noise: float32 [16, 1024], P(None, 'tp'), may hold values from -4 to 4
Outputs:
- qdown_gmean: float32 [16, 8192], P(None, 'tp')
- qdown_gsigma: float32 [16, 8192], P(None, 'tp')
- qup_gmean: float32 [16, 4096], P(None, 'tp')
- qup_gsigma: float32 [16, 4096], P(None, 'tp')
- vdown_gmean: float32 [16, 8192], P(None, 'tp')
- vdown_gsigma: float32 [16, 8192], P(None, 'tp')
- vup_gmean: float32 [16, 1024], P(None, 'tp')
- vup_gsigma: float32 [16, 1024], P(None, 'tp')
The draws below stay inside these ranges and needn't reach their ends.
All inputs are finite; a program needn't handle non-finite values.
Results may differ from the reference program's by a relative error of at most 0.0075.
The reference program's roundings to bfloat16 on the way count: a program that leaves them out, or rounds other values in their place, can miss the bound.
Values may be sent and summed in bfloat16 or wider, within the bound.
No kernel may reach another device: no remote copies, remote signals or barrier semaphores. Data moves between devices by JAX's collectives and lax.ppermute only.
A program may use at most 64 MiB of HBM per device.

```python
import math
import jax
import jax.numpy as jnp
from jax import lax

D = 8192
QUERY_HEADS = 32
KEY_VALUE_HEADS = 8
HEAD_SIZE = 128
ADAPTER_RANK = 16
SEQUENCE_LENGTH = 8192


def joint_draw(key):
    key_portion = jnp.clip(jax.random.normal(jax.random.fold_in(key, 7101), (SEQUENCE_LENGTH, KEY_VALUE_HEADS * HEAD_SIZE), jnp.float32), -6.0, 6.0)
    query_part = jnp.clip(jax.random.normal(jax.random.fold_in(key, 7102), (SEQUENCE_LENGTH, QUERY_HEADS * HEAD_SIZE), jnp.float32), -6.0, 6.0)
    return (query_part, key_portion)


def draw_query_base(key, part):
    return joint_draw(key)[0].astype(jnp.bfloat16)


def draw_rotated_key_cache(key, part):
    return joint_draw(key)[1].astype(jnp.bfloat16)


def draw_output_cotangent(key, part):
    along = jnp.arange(SEQUENCE_LENGTH, dtype=jnp.float32) / (SEQUENCE_LENGTH - 1.0)
    ramp = 1.0 + 2.0 * along
    values = jnp.clip(jax.random.normal(jax.random.fold_in(key, 7201), (SEQUENCE_LENGTH, QUERY_HEADS * HEAD_SIZE), jnp.float32), -6.0, 6.0)
    result = 0.05 * values * ramp[:, None]
    return result.astype(jnp.bfloat16)


def levels(own_key, dims, split, smallest, top_value):
    def one(dim, blocks):
        heights = jax.random.uniform(jax.random.fold_in(jax.random.fold_in(own_key, 6), dim), (blocks,), jnp.float32, smallest / len(split), top_value / len(split))
        return jnp.repeat(jnp.exp(heights), dims[dim] // blocks).reshape((-1,) + (1,) * (len(dims) - dim - 1))

    loudness = one(*split[0])
    for cut in split[1:]:
        loudness = loudness * one(*cut)
    return loudness


def gaussian(rng, extent, scale, reach, pieces=(), kind=jnp.bfloat16):
    values = jax.random.normal(rng, extent, jnp.float32) * scale
    if len(pieces) > 0:
        values = levels(rng, extent, pieces, -0.22, 0.18) * values
    return jnp.clip(values, min=-reach, max=reach).astype(kind)


def setup_inputs(seed: int = 0) -> dict:
    arg_keys = jax.random.split(jax.random.key(seed), 18)
    return {
        "hidden": gaussian(arg_keys[0], (SEQUENCE_LENGTH, D), 1.0, 6.0, ((0, 32), (1, 8))),
        "query_base": draw_query_base(jax.random.fold_in(arg_keys[17], 71), 0),
        "rotated_key_cache": draw_rotated_key_cache(jax.random.fold_in(arg_keys[17], 71), 0),
        "frozen_value_base": gaussian(arg_keys[3], (SEQUENCE_LENGTH, KEY_VALUE_HEADS * HEAD_SIZE), 1.0, 6.0, ((0, 32), (1, 8))),
        "output_cotangent": draw_output_cotangent(jax.random.fold_in(arg_keys[17], 71), 0),
        "qdown_mean": gaussian(arg_keys[5], (ADAPTER_RANK, D), D ** -0.5, 0.0625, ((1, 8),), jnp.float32),
        "qdown_sigma": jnp.clip(jnp.exp(math.log(0.012) - 1.09861225 * jax.random.uniform(arg_keys[6], (ADAPTER_RANK, D), jnp.float32) ** levels(arg_keys[6], (ADAPTER_RANK, D), ((1, 8),), -0.2, 0.2)), 0.004, 0.012),
        "qdown_noise": gaussian(arg_keys[7], (ADAPTER_RANK, D), 1.0, 4.0, ((1, 8),), jnp.float32),
        "qup_mean": gaussian(arg_keys[8], (ADAPTER_RANK, QUERY_HEADS * HEAD_SIZE), ADAPTER_RANK ** -0.5, 1.5, ((1, 8),), jnp.float32),
        "qup_sigma": jnp.clip(jnp.exp(math.log(0.25) - 1.1394343 * jax.random.uniform(arg_keys[9], (ADAPTER_RANK, QUERY_HEADS * HEAD_SIZE), jnp.float32) ** levels(arg_keys[9], (ADAPTER_RANK, QUERY_HEADS * HEAD_SIZE), ((1, 8),), -0.2, 0.2)), 0.08, 0.25),
        "qup_noise": gaussian(arg_keys[10], (ADAPTER_RANK, QUERY_HEADS * HEAD_SIZE), 1.0, 4.0, ((1, 8),), jnp.float32),
        "vdown_mean": gaussian(arg_keys[11], (ADAPTER_RANK, D), D ** -0.5, 0.0625, ((1, 8),), jnp.float32),
        "vdown_sigma": jnp.clip(jnp.exp(math.log(0.012) - 1.09861225 * jax.random.uniform(arg_keys[12], (ADAPTER_RANK, D), jnp.float32) ** levels(arg_keys[12], (ADAPTER_RANK, D), ((1, 8),), -0.2, 0.2)), 0.004, 0.012),
        "vdown_noise": gaussian(arg_keys[13], (ADAPTER_RANK, D), 1.0, 4.0, ((1, 8),), jnp.float32),
        "value_up_mean": gaussian(arg_keys[14], (ADAPTER_RANK, KEY_VALUE_HEADS * HEAD_SIZE), ADAPTER_RANK ** -0.5, 1.5, ((1, 8),), jnp.float32),
        "value_up_deviation": jnp.clip(jnp.exp(math.log(0.25) - 1.1394343 * jax.random.uniform(arg_keys[15], (ADAPTER_RANK, KEY_VALUE_HEADS * HEAD_SIZE), jnp.float32) ** levels(arg_keys[15], (ADAPTER_RANK, KEY_VALUE_HEADS * HEAD_SIZE), ((1, 8),), -0.2, 0.2)), 0.08, 0.25),
        "value_up_noise": gaussian(arg_keys[16], (ADAPTER_RANK, KEY_VALUE_HEADS * HEAD_SIZE), 1.0, 4.0, ((1, 8),), jnp.float32),
    }


def sample(mean, sigma, noise):
    return (mean + sigma * noise).astype(jnp.bfloat16)


def head_grads(query_g, key_g, value_g, grad_g):
    query_group = QUERY_HEADS // KEY_VALUE_HEADS
    scale = HEAD_SIZE ** -0.5
    qblock = math.gcd(SEQUENCE_LENGTH, 512)
    blocks = SEQUENCE_LENGTH // qblock
    key_pos = jnp.arange(SEQUENCE_LENGTH, dtype=jnp.int32)

    def advance(dv_acc, index):
        start = (index * qblock).astype(jnp.int32)
        rows_q = lax.dynamic_slice_in_dim(query_g, start, qblock, 0).reshape(qblock * query_group, HEAD_SIZE)
        rows_d = lax.dynamic_slice_in_dim(grad_g, start, qblock, 0).reshape(qblock * query_group, HEAD_SIZE)
        row_pos = start + jnp.arange(qblock * query_group, dtype=jnp.int32) // query_group
        mask = key_pos[None, :] <= row_pos[:, None]
        scores = jnp.dot(rows_q, key_g.T, preferred_element_type=jnp.float32) * scale
        masked = jnp.where(mask, scores, -jnp.inf)
        top = jnp.max(masked, axis=1, keepdims=True)
        total = jnp.sum(jnp.exp(masked - top), axis=1, keepdims=True)
        lse = top + jnp.log(total)
        probs = jnp.exp(masked - lse)
        dprob = jnp.dot(rows_d, value_g.T, preferred_element_type=jnp.float32)
        delta = jnp.sum(probs * dprob, axis=1, keepdims=True)
        dscore = (probs * (dprob - delta)).astype(jnp.bfloat16)
        dquery = (jnp.dot(dscore, key_g, preferred_element_type=jnp.float32) * scale).astype(jnp.bfloat16)
        dv_acc = dv_acc + jnp.dot(probs.astype(jnp.bfloat16).T, rows_d, preferred_element_type=jnp.float32)
        return dv_acc, dquery.reshape(qblock, query_group * HEAD_SIZE)

    dv_acc, dq_blocks = lax.scan(advance, jnp.zeros((SEQUENCE_LENGTH, HEAD_SIZE), jnp.float32), jnp.arange(blocks, dtype=jnp.int32))
    return dq_blocks.reshape(SEQUENCE_LENGTH, query_group * HEAD_SIZE), dv_acc.astype(jnp.bfloat16)


def reference(hidden, query_base, rotated_key_cache, frozen_value_base, output_cotangent, qdown_mean, qdown_sigma, qdown_noise, qup_mean, qup_sigma, qup_noise, vdown_mean, vdown_sigma, vdown_noise, value_up_mean, value_up_deviation, value_up_noise):
    query_group = QUERY_HEADS // KEY_VALUE_HEADS
    qdown = sample(qdown_mean, qdown_sigma, qdown_noise)
    qup = sample(qup_mean, qup_sigma, qup_noise)
    vdown = sample(vdown_mean, vdown_sigma, vdown_noise)
    vup = sample(value_up_mean, value_up_deviation, value_up_noise)
    qlow = jnp.dot(hidden, qdown.T, preferred_element_type=jnp.float32).astype(jnp.bfloat16)
    vlow = jnp.dot(hidden, vdown.T, preferred_element_type=jnp.float32).astype(jnp.bfloat16)
    query_input = (query_base.astype(jnp.float32) + jnp.dot(qlow, qup, preferred_element_type=jnp.float32)).astype(jnp.bfloat16)
    value_input = (frozen_value_base.astype(jnp.float32) + jnp.dot(vlow, vup, preferred_element_type=jnp.float32)).astype(jnp.bfloat16)
    head_queries = query_input.reshape(SEQUENCE_LENGTH, KEY_VALUE_HEADS, query_group * HEAD_SIZE).transpose(1, 0, 2)
    head_output_gradient = output_cotangent.reshape(SEQUENCE_LENGTH, KEY_VALUE_HEADS, query_group * HEAD_SIZE).transpose(1, 0, 2)
    head_keys = rotated_key_cache.reshape(SEQUENCE_LENGTH, KEY_VALUE_HEADS, HEAD_SIZE).transpose(1, 0, 2)
    head_values = value_input.reshape(SEQUENCE_LENGTH, KEY_VALUE_HEADS, HEAD_SIZE).transpose(1, 0, 2)
    dq_h, value_head_gradient = lax.map(lambda items: head_grads(items[0], items[1], items[2], items[3]), (head_queries, head_keys, head_values, head_output_gradient))
    dquery = dq_h.transpose(1, 0, 2).reshape(SEQUENCE_LENGTH, QUERY_HEADS * HEAD_SIZE)
    value_gradient = value_head_gradient.transpose(1, 0, 2).reshape(SEQUENCE_LENGTH, KEY_VALUE_HEADS * HEAD_SIZE)
    qup_grad = jnp.dot(qlow.T, dquery, preferred_element_type=jnp.float32)
    vup_grad = jnp.dot(vlow.T, value_gradient, preferred_element_type=jnp.float32)
    qlow_grad = jnp.dot(dquery, qup.T, preferred_element_type=jnp.float32).astype(jnp.bfloat16)
    vlow_grad = jnp.dot(value_gradient, vup.T, preferred_element_type=jnp.float32).astype(jnp.bfloat16)
    qdown_grad = jnp.dot(qlow_grad.T, hidden, preferred_element_type=jnp.float32)
    vdown_grad = jnp.dot(vlow_grad.T, hidden, preferred_element_type=jnp.float32)
    return (qdown_grad, qdown_grad * qdown_noise, qup_grad, qup_grad * qup_noise, vdown_grad, vdown_grad * vdown_noise, vup_grad, vup_grad * value_up_noise)
```

```python
import functools

import jax
import jax.numpy as jnp
from jax import lax
from jax.experimental import pallas as pl
from jax.experimental.pallas import tpu as pltpu
from jax.sharding import Mesh
from jax.sharding import PartitionSpec as P


HEAD_SIZE = 128
RANK = 16
GROUP = 4
BLOCK = 256
NZ, NX = 8, 4
SCALE = HEAD_SIZE**-0.5
LOG2E = 1.4426950408889634
EMPTY = -1e30
NT = (((1,), (1,)), ((), ()))


def sample(mean, sigma, noise):
    return (mean + sigma * noise).astype(jnp.bfloat16)


def dot(a, b, dims=(((1,), (0,)), ((), ()))):
    return lax.dot_general(a, b, dims, preferred_element_type=jnp.float32)


def pair(n, z, x):
    late = n >= 4 * z
    kz = jnp.where(late, z, n // 4)
    k = jnp.where(late, x + 1 + n - 4 * z, lax.rem(n, 4))
    return kz, k


def head(ref, k, h):
    return ref[k, 0:BLOCK, h * HEAD_SIZE : (h + 1) * HEAD_SIZE]


def causal():
    keys = lax.broadcasted_iota(jnp.int32, (BLOCK, BLOCK), 0)
    rows = lax.broadcasted_iota(jnp.int32, (BLOCK, BLOCK), 1)
    return keys <= rows


def stats_kernel(pos_ref, q_ref, do_ref, kv_ref, out_ref, state):
    z, x = pos_ref[0], pos_ref[1]
    for k in range(NX):
        for h in range(GROUP):
            state[k, h, 0] = jnp.full((8, BLOCK), EMPTY, jnp.float32)
            state[k, h, 1] = jnp.zeros((8, BLOCK), jnp.float32)
            state[k, h, 2] = jnp.zeros((8, BLOCK), jnp.float32)

    def step(kz, k, masked):
        keys = kv_ref[kz, 0:BLOCK, 0:HEAD_SIZE]
        values = kv_ref[kz, 0:BLOCK, HEAD_SIZE : 2 * HEAD_SIZE]
        for h in range(GROUP):
            score = dot(keys, head(q_ref, k, h), NT) * (SCALE * LOG2E)
            dprob = dot(values, head(do_ref, k, h), NT).reshape(BLOCK // 8, 8, BLOCK)
            if masked:
                mask = causal()
                score = jnp.where(mask, score, EMPTY)
            score = score.reshape(BLOCK // 8, 8, BLOCK)
            top, total, weighted = state[k, h, 0], state[k, h, 1], state[k, h, 2]
            fresh = jnp.maximum(top, jnp.max(score, axis=0))
            weights = jnp.exp2(score - fresh[None])
            if masked:
                weights = jnp.where(mask.reshape(BLOCK // 8, 8, BLOCK), weights, 0.0)
            decay = jnp.exp2(top - fresh)
            state[k, h, 0] = fresh
            state[k, h, 1] = total * decay + jnp.sum(weights, axis=0)
            state[k, h, 2] = weighted * decay + jnp.sum(weights * dprob, axis=0)

    def whole(n, carry):
        kz, k = pair(n, z, x)
        step(kz, k, False)
        return carry

    lax.fori_loop(0, 4 * z + 3 - x, whole, 0)
    step(z, 0, True)
    for k in range(NX):
        source = lax.rem(x + NX - k, NX)
        for h in range(GROUP):
            top, total, weighted = state[k, h, 0], state[k, h, 1], state[k, h, 2]
            most = jnp.max(top, axis=0, keepdims=True)
            decay = jnp.exp2(top - most)
            out_ref[source, h : h + 1, :] = most
            out_ref[source, 4 + h : 5 + h, :] = jnp.sum(total * decay, axis=0, keepdims=True)
            out_ref[source, 8 + h : 9 + h, :] = jnp.sum(weighted * decay, axis=0, keepdims=True)
        out_ref[source, 12:16, :] = jnp.zeros((4, BLOCK), jnp.float32)


def grads_kernel(
    pos_ref, stats_ref, q_ref, do_ref, kv_ref, qup_ref, vup_ref,
    dqlow_ref, dvlow_ref, up_ref, keys_t, dquery, dvalue, rows,
):
    z, x = pos_ref[0], pos_ref[1]
    for k in range(NX):
        source = lax.rem(x + NX - k, NX)
        tops = [stats_ref[i, source, 0:4, :] for i in range(NX)]
        most = functools.reduce(jnp.maximum, tops)
        decays = [jnp.exp2(top - most) for top in tops]
        total = sum(stats_ref[i, source, 4:8, :] * decays[i] for i in range(NX))
        weighted = sum(stats_ref[i, source, 8:12, :] * decays[i] for i in range(NX))
        rows[k, 0:4, :] = most + jnp.log2(total)
        rows[k, 4:8, :] = weighted / total
    dquery[...] = jnp.zeros_like(dquery)
    dvalue[...] = jnp.zeros_like(dvalue)
    keys_t[...] = jnp.zeros_like(keys_t)

    def flip(kz, carry):
        keys_t[kz] = kv_ref[kz, 0:BLOCK, 0:HEAD_SIZE].T
        return carry

    lax.fori_loop(0, z + 1, flip, 0)

    def step(kz, k, masked):
        keys = kv_ref[kz, 0:BLOCK, 0:HEAD_SIZE]
        values = kv_ref[kz, 0:BLOCK, HEAD_SIZE : 2 * HEAD_SIZE]
        flipped = keys_t[kz]
        value_sum = dvalue[kz]
        for h in range(GROUP):
            cotangent = head(do_ref, k, h)
            score = dot(keys, head(q_ref, k, h), NT) * (SCALE * LOG2E)
            dprob = dot(values, cotangent, NT)
            prob = jnp.exp2(score - rows[k, h : h + 1, :])
            if masked:
                prob = jnp.where(causal(), prob, 0.0)
            dscore = (prob * (dprob - rows[k, 4 + h : 5 + h, :])).astype(jnp.bfloat16)
            dquery[k, h] += dot(flipped, dscore)
            value_sum = value_sum + dot(prob.astype(jnp.bfloat16), cotangent)
        dvalue[kz] = value_sum

    def whole(n, carry):
        kz, k = pair(n, z, x)
        step(kz, k, False)
        return carry

    lax.fori_loop(0, 4 * z + 3 - x, whole, 0)
    step(z, 0, True)

    up = [jnp.zeros((RANK, HEAD_SIZE), jnp.float32) for _ in range(GROUP + 1)]
    for k in range(NX):
        qlow = q_ref[k, BLOCK : BLOCK + RANK, 0:BLOCK]
        low = jnp.zeros((RANK, BLOCK), jnp.float32)
        for h in range(GROUP):
            part = (dquery[k, h] * SCALE).astype(jnp.bfloat16)
            low = low + dot(qup_ref[:, h * HEAD_SIZE : (h + 1) * HEAD_SIZE], part)
            up[h] = up[h] + dot(qlow, part, NT)
        dqlow_ref[k] = low
    for kz in range(NZ):
        part = dvalue[kz].astype(jnp.bfloat16)
        dvlow_ref[kz] = dot(vup_ref[...], part, NT)
        up[GROUP] = up[GROUP] + dot(kv_ref[kz, BLOCK : BLOCK + RANK, 0:BLOCK], part)
    for i in range(GROUP + 1):
        up_ref[i] = up[i]
    up_ref[5:8] = jnp.zeros((3, RANK, HEAD_SIZE), jnp.float32)


def spread(value, axis, size):
    copies = jnp.broadcast_to(value[None], (size,) + value.shape)
    return lax.all_to_all(copies, axis, 0, 0, tiled=True)


def along_x(value, step):
    return [
        lax.ppermute(value, "x", [(i, (i + step * k) % NX) for i in range(NX)]) for k in (1, 2, 3)
    ]


def per_device(
    hidden,
    query_base,
    rotated_key_cache,
    frozen_value_base,
    output_cotangent,
    qdown_mean,
    qdown_sigma,
    qdown_noise,
    qup_mean,
    qup_sigma,
    qup_noise,
    vdown_mean,
    vdown_sigma,
    vdown_noise,
    value_up_mean,
    value_up_deviation,
    value_up_noise,
):
    bf16, f32 = jnp.bfloat16, jnp.float32
    z, x = lax.axis_index("z"), lax.axis_index("x")
    pos = jnp.stack([z, x]).astype(jnp.int32)
    cotangents = jnp.stack([output_cotangent] + along_x(output_cotangent, 1))
    down = jnp.concatenate(
        [sample(qdown_mean, qdown_sigma, qdown_noise), sample(vdown_mean, vdown_sigma, vdown_noise)]
    )
    qup = sample(qup_mean, qup_sigma, qup_noise)
    vup = sample(value_up_mean, value_up_deviation, value_up_noise)
    parts = dot(down, hidden, NT)
    low = jnp.sum(spread(parts, "tp", 8), axis=0).astype(bf16)
    qlow, vlow = low[:RANK], low[RANK:]
    query = (query_base.astype(f32) + dot(qlow, qup, (((0,), (0,)), ((), ())))).astype(bf16)
    value = (frozen_value_base.astype(f32) + dot(vlow, vup, (((0,), (0,)), ((), ())))).astype(bf16)
    query_pack = jnp.concatenate([query, jnp.pad(qlow, ((0, 0), (0, BLOCK)))])
    key_pack = jnp.concatenate([jnp.concatenate([rotated_key_cache, value], axis=1), vlow])
    queries = jnp.stack([query_pack] + along_x(query_pack, 1))
    keys = spread(key_pack, "z", NZ)

    vmem = pl.BlockSpec(memory_space=pltpu.VMEM)
    smem = pl.BlockSpec(memory_space=pltpu.SMEM)
    stats = pl.pallas_call(
        stats_kernel,
        out_shape=jax.ShapeDtypeStruct((NX, 16, BLOCK), f32),
        in_specs=[smem, vmem, vmem, vmem],
        out_specs=vmem,
        scratch_shapes=[pltpu.VMEM((NX, GROUP, 3, 8, BLOCK), f32)],
        name="stats",
    )(pos, queries, cotangents, keys)
    stats = spread(stats, "x", NX)
    dqlow, dvlow, ups = pl.pallas_call(
        grads_kernel,
        out_shape=(
            jax.ShapeDtypeStruct((NX, RANK, BLOCK), f32),
            jax.ShapeDtypeStruct((NZ, RANK, BLOCK), f32),
            jax.ShapeDtypeStruct((NZ, RANK, HEAD_SIZE), f32),
        ),
        in_specs=[smem] + [vmem] * 6,
        out_specs=(vmem, vmem, vmem),
        scratch_shapes=[
            pltpu.VMEM((NZ, HEAD_SIZE, BLOCK), bf16),
            pltpu.VMEM((NX, GROUP, HEAD_SIZE, BLOCK), f32),
            pltpu.VMEM((NZ, BLOCK, HEAD_SIZE), f32),
            pltpu.VMEM((NX, 8, BLOCK), f32),
        ],
        name="grads",
    )(pos, stats, queries, cotangents, keys, qup, vup)

    back = [
        lax.ppermute(dqlow[k], "x", [(i, (i - k) % NX) for i in range(NX)]) for k in (1, 2, 3)
    ]
    vlow_grad = jnp.sum(lax.all_to_all(dvlow, "z", 0, 0, tiled=True), axis=0)
    qlow_grad = dqlow[0] + back[0] + back[1] + back[2]
    low_grad = jnp.concatenate([qlow_grad, vlow_grad])
    low_grad = jnp.sum(spread(low_grad, "tp", 8), axis=0).astype(bf16)
    down_grad = dot(low_grad, hidden)
    pieces = down_grad.reshape(2 * RANK, NZ, HEAD_SIZE).transpose(1, 0, 2)
    pieces = jnp.concatenate([pieces, ups], axis=1)
    piece = jnp.sum(lax.all_to_all(pieces, "z", 0, 0, tiled=True), axis=0)
    piece = jnp.sum(spread(piece, "x", NX), axis=0)
    pieces = spread(piece, "z", NZ)
    pieces = pieces.transpose(1, 0, 2).reshape(3 * RANK, NZ * HEAD_SIZE)
    qdown_grad, vdown_grad = pieces[:RANK], pieces[RANK : 2 * RANK]
    qup_grad = pieces[2 * RANK :, : GROUP * HEAD_SIZE]
    vup_grad = pieces[2 * RANK :, GROUP * HEAD_SIZE : (GROUP + 1) * HEAD_SIZE]
    return (
        qdown_grad,
        qdown_grad * qdown_noise,
        qup_grad,
        qup_grad * qup_noise,
        vdown_grad,
        vdown_grad * vdown_noise,
        vup_grad,
        vup_grad * value_up_noise,
    )


def solution(mesh):
    fine = Mesh(mesh.devices.reshape(NZ, NX, 8), ("z", "x", "tp"))
    tokens = P(("z", "x"), "tp")
    return jax.shard_map(
        per_device,
        mesh=fine,
        in_specs=(tokens,) * 5 + (P(None, "tp"),) * 12,
        out_specs=(P(None, "tp"),) * 8,
        check_vma=False,
    )
```
